32 devices in a mesh: beam: 2 (over y), freq: 8 (over z, x), tm: 2 (over core).
Axes of the slice: x: 2, y: 2, z: 4, core: 2. Of those that a mesh axis runs over, the one named last changes fastest.
Arguments:
- spectra: float32 [256, 16384], P(('beam', 'freq'), 'tm'), parts along dimension 0, may hold values from -250 to 250
- local_delays: int32 [4, 3, 128], P(None, None, 'freq'), may hold values from 0 to 8, as said below
- merge_delays: int32 [3, 3, 128], P(None, None, 'freq'), may hold values from 0 to 64, as said below
- widths: int32 [16], replicated, may hold values from 1 to 32, as said below
Outputs:
- detections: float32 [256, 16384], P(('beam', 'freq'), 'tm'), parts along dimension 0
The draws below stay inside these ranges and needn't reach their ends.
There are 2 independent parts, one for each index of `beam`. The reference program is written for one: setup_inputs(seed, part) draws one part's arguments, and reference() takes and returns one part's arrays. A program takes and returns all parts, laid end to end along the dimension named above; an argument that names none is the same for every part. Nothing has to cross between parts.
Inputs may be any that keep to these rules, and one draw needn't show every extreme that they name: `local_delays`: entries [s, 0, r] and [s, 1, r] lie in 0 to 2**s - 1, entry [s, 2, r] in 0 to 2**s, and [s, 2, 0] equals 2**s. `merge_delays`: entries [j, 0, r] and [j, 1, r] lie in 0 to 15, entry [j, 2, r] in 0 to 16 * 2**j, and [j, 2, 0] equals 16 * 2**j. 16 distinct widths, one of them 32.
All inputs are finite; a program needn't handle non-finite values.
Results may differ from the reference program's by a relative error of at most 0.00002.
Values sent between devices are 32-bit elements; how exact they have to be, the bound alone decides.
A program may use at most 64 MiB of HBM per device.

```python
import math
import jax
import jax.numpy as jnp
from jax import lax

CH_DEV = 16
LLEVELS = 4
BLEVELS = 3
CHANNELS = 128
TIMES = 16384
WMAX = 32
NWIDTH = 16


def draw_spectra(key, part):
    subkeys = jax.random.split(key, 3)
    fraction = jnp.arange(TIMES, dtype=jnp.float32) / TIMES
    noise_part = jnp.clip(jax.random.normal(subkeys[0], (CHANNELS, TIMES), jnp.float32), -5.0, 5.0)
    channel_gain = jnp.exp(jax.random.uniform(subkeys[1], (CHANNELS, 1), jnp.float32, 0.0, math.log(10.0)))
    baseline = jax.random.uniform(subkeys[2], (CHANNELS, 1), jnp.float32, -2.0, 2.0)
    return channel_gain * (noise_part * (0.5 + fraction) + baseline * 3.0 * fraction)


def draw_local_delays(key, part):
    subkeys = jax.random.split(key, 3)
    level_size = (2 ** jnp.arange(LLEVELS, dtype=jnp.int32))[:, None]
    low_pick = jax.random.randint(subkeys[0], (LLEVELS, CHANNELS), 0, level_size)
    high_pick = jax.random.randint(subkeys[1], (LLEVELS, CHANNELS), 0, level_size)
    lag_table = jax.random.randint(subkeys[2], (LLEVELS, CHANNELS), 0, level_size + 1)
    lag_table = lag_table.at[:, 0].set(level_size[:, 0])
    return jnp.stack([low_pick, high_pick, lag_table], axis=1).astype(jnp.int32)


def draw_merge_delays(key, part):
    subkeys = jax.random.split(key, 3)
    level_size = (CH_DEV * 2 ** jnp.arange(BLEVELS, dtype=jnp.int32))[:, None]
    low_pick = jax.random.randint(subkeys[0], (BLEVELS, CHANNELS), 0, CH_DEV)
    high_pick = jax.random.randint(subkeys[1], (BLEVELS, CHANNELS), 0, CH_DEV)
    lag_table = jax.random.randint(subkeys[2], (BLEVELS, CHANNELS), 0, level_size + 1)
    lag_table = lag_table.at[:, 0].set(level_size[:, 0])
    return jnp.stack([low_pick, high_pick, lag_table], axis=1).astype(jnp.int32)


def draw_widths(key, part):
    shuffled = jax.random.permutation(key, WMAX - 1) + 1
    return jnp.concatenate([shuffled[:NWIDTH - 1], jnp.array([WMAX])]).astype(jnp.int32)


def setup_inputs(seed: int = 0, part: int = 0) -> dict:
    splits = jax.random.split(jax.random.key(seed), 5)
    part_keys = jax.random.split(jax.random.fold_in(splits[4], part), 5)
    return {
        "spectra": draw_spectra(jax.random.fold_in(jax.random.fold_in(splits[4], part), 71), part),
        "local_delays": draw_local_delays(jax.random.fold_in(splits[4], 71), part),
        "merge_delays": draw_merge_delays(jax.random.fold_in(splits[4], 71), part),
        "widths": draw_widths(jax.random.fold_in(splits[4], 71), part),
    }


EPSILON = 1e-05

def shift_rows(signal, delays, length):
    return jax.vmap(lambda one_row, one_lag: lax.dynamic_slice_in_dim(one_row, one_lag, length))(signal, delays)

def reference(spectra, local_delays, merge_delays, widths):
    average = lax.optimization_barrier(jnp.mean(spectra, axis=1, keepdims=True))
    centered = spectra - average
    variance = lax.optimization_barrier(jnp.mean(centered * centered, axis=1, keepdims=True))
    series = centered / jnp.sqrt(variance + EPSILON)
    row_ids = jnp.arange(CHANNELS, dtype=jnp.int32)
    for level_num in range(LLEVELS):
        level_size = 2 ** level_num
        base_row = row_ids // (2 * level_size) * (2 * level_size)
        low_rows = series[base_row + local_delays[level_num, 0]]
        high_rows = jnp.pad(series[base_row + level_size + local_delays[level_num, 1]], ((0, 0), (0, level_size)))
        series = low_rows + shift_rows(high_rows, local_delays[level_num, 2], TIMES)
    device_ids = row_ids // CH_DEV
    for level_num in range(BLEVELS):
        stride = 2 ** level_num
        low_device = device_ids - device_ids // stride % 2 * stride
        low_rows = series[low_device * CH_DEV + merge_delays[level_num, 0]]
        high_rows = series[(low_device + stride) * CH_DEV + merge_delays[level_num, 1]]
        high_rows = jnp.pad(high_rows, ((0, 0), (0, CH_DEV * stride)))
        series = low_rows + shift_rows(high_rows, merge_delays[level_num, 2], TIMES)
    extended = jnp.pad(series, ((0, 0), (0, WMAX - 1)))
    running = jnp.zeros((CHANNELS, TIMES), jnp.float32)
    strongest = jnp.full((CHANNELS, TIMES), -jnp.inf, jnp.float32)
    for offset in range(WMAX):
        running = running + extended[:, offset:offset + TIMES]
        chosen = jnp.any(widths == offset + 1)
        strongest = jnp.where(chosen, jnp.maximum(strongest, running * (1.0 / math.sqrt(offset + 1))), strongest)
    return strongest * (1.0 / math.sqrt(CHANNELS))
```

```python
import functools
import math

import jax
import jax.numpy as jnp
from jax import lax
from jax.experimental import pallas as pl
from jax.experimental.pallas import tpu as pltpu
from jax.sharding import PartitionSpec as P

WMAX = 32
EPSILON = 1e-05
LANES = 128
SUB = 8
MESH = pl.DeviceIdType.MESH
FIRST_LAG = 1
MID_LAG = 1
LAST_LAG = 3


def kernel(geo, x_ref, ld_ref, md_ref, w_ref, o_ref, *scratch):
    channels, chunks, freq_count, halo_chunks, tile = geo
    groups = channels // SUB
    llevels = channels.bit_length() - 1
    flevels = freq_count.bit_length() - 1
    samples = chunks * LANES
    nwidth = w_ref.shape[0]
    halo, st_own, st_peer, nrm, fin, eb, tri, scl = scratch[:8]
    loc = scratch[8 : 8 + llevels]
    count = chunks // tile
    flat_bufs = scratch[8 + llevels : 8 + llevels + flevels * count]
    bufs = [flat_bufs[j * count : (j + 1) * count] for j in range(flevels)]
    hsend, hrecv, ssend, srecv, bsend, brecv = scratch[8 + llevels + flevels * count :]

    tm = lax.axis_index("tm")
    freq = lax.axis_index("freq")
    peer = {"tm": 1 - tm}
    sides, partners = [], []
    for j in range(flevels):
        stride = 2**j
        side = (freq // stride) % 2
        sides.append(side)
        partners.append({"freq": freq + stride - 2 * stride * side})

    barrier = pltpu.get_barrier_semaphore()
    for other in [peer] + partners:
        pl.semaphore_signal(barrier, inc=1, device_id=other, device_id_type=MESH)

    lane = lax.broadcasted_iota(jnp.int32, (SUB, LANES), 1)

    for g in range(groups):
        block = x_ref[pl.ds(g * chunks * SUB, chunks * SUB), :].reshape(chunks, SUB, LANES)
        mean = jnp.sum(jnp.sum(block, axis=0), axis=1, keepdims=True) / samples
        off = block - mean[None]
        square = jnp.sum(jnp.sum(off * off, axis=0), axis=1, keepdims=True)
        st_own[0, pl.ds(g * SUB, SUB), :] = jnp.broadcast_to(mean, (SUB, LANES))
        st_own[1, pl.ds(g * SUB, SUB), :] = jnp.broadcast_to(square, (SUB, LANES))

    pl.semaphore_wait(barrier, 1 + flevels)
    stat_copy = pltpu.make_async_remote_copy(
        src_ref=st_own, dst_ref=st_peer, send_sem=ssend, recv_sem=srecv,
        device_id=peer, device_id_type=MESH,
    )
    stat_copy.start()
    halo_copies = []
    for g in range(groups):
        copy = pltpu.make_async_remote_copy(
            src_ref=x_ref.at[pl.ds(g * chunks * SUB, halo_chunks * SUB), :],
            dst_ref=halo.at[g],
            send_sem=hsend.at[g], recv_sem=hrecv.at[g],
            device_id=peer, device_id_type=MESH,
        )
        copy.start()
        halo_copies.append(copy)

    before = lax.broadcasted_iota(jnp.int32, (LANES, 2 * LANES), 0)
    after = lax.broadcasted_iota(jnp.int32, (LANES, 2 * LANES), 1)
    tri[...] = jnp.where(before < after, 1.0, 0.0)
    norm = 1.0 / math.sqrt(channels * freq_count)
    for i in range(nwidth):
        wide = jnp.full((SUB, LANES), w_ref[i].astype(jnp.float32), jnp.float32)
        scl[i] = (1.0 / jnp.sqrt(wide)) * norm

    stat_copy.wait_recv()
    mean_a, mean_b = st_own[0], st_peer[0]
    gap = mean_a - mean_b
    variance = (st_own[1] + st_peer[1] + gap * gap * (samples / 2)) / (2 * samples)
    nrm[0] = (mean_a + mean_b) * 0.5
    nrm[1] = 1.0 / jnp.sqrt(variance + EPSILON)
    for copy in halo_copies:
        copy.wait_recv()

    keep = jnp.where(tm == 0, 1.0, 0.0)

    def rows(body):
        def step(g, carry):
            body(g)
            return carry

        lax.fori_loop(0, groups, step, 0)

    def normalise(c0, size, is_halo):
        def body(g):
            out = []
            for i in range(SUB):
                r = g * SUB + i
                if is_halo:
                    part = halo[g, pl.ds(i, halo_chunks, stride=SUB), :]
                    gain = nrm[1, pl.ds(r, 1), :] * keep
                else:
                    part = x_ref[pl.ds(g * chunks * SUB + c0 * SUB + i, size, stride=SUB), :]
                    gain = nrm[1, pl.ds(r, 1), :]
                out.append((part - nrm[0, pl.ds(r, 1), :]) * gain)
            for i in range(SUB):
                r = g * SUB + i
                count = halo_chunks if is_halo else size
                loc[0][r, pl.ds(c0, count), :] = out[i]

        rows(body)

    def merged(low, high, lag, span, c0, size):
        if span < LANES:
            jump = 0
        else:
            jump = lag // LANES
            lag = lag % LANES
        cur = high(c0 + jump, size)
        nxt = high(c0 + jump + 1, size)
        lanes = lax.broadcasted_iota(jnp.int32, (size, LANES), 1)
        mixed = jnp.where(lanes < lag, nxt, cur)
        return low(c0, size) + pltpu.roll(mixed, (LANES - lag) % LANES, 1)

    def put(level, k, r, rel, size, value):
        bufs[level][k][sides[level], r, pl.ds(rel, size), :] = value

    def local_level(s, k, c0, size):
        span = 2**s
        src = loc[s]

        def body(g):
            out = []
            for i in range(SUB):
                r = g * SUB + i
                base = (r // (2 * span)) * (2 * span)
                lo_row = base + ld_ref[s, 0, r]
                hi_row = base + span + ld_ref[s, 1, r]
                out.append(merged(
                    lambda c, n: src[lo_row, pl.ds(c, n), :],
                    lambda c, n: src[hi_row, pl.ds(c, n), :],
                    ld_ref[s, 2, r], span, c0, size,
                ))
            for i in range(SUB):
                r = g * SUB + i
                if s + 1 < llevels:
                    loc[s + 1][r, pl.ds(c0, size), :] = out[i]
                else:
                    put(0, k, r, c0 - pieces[k][0], size, out[i])

        rows(body)

    def merge_level(j, k, c0, size):
        span = channels * 2**j
        src = bufs[j][k]

        def body(g):
            out = []
            for i in range(SUB):
                r = g * SUB + i
                lo_row = md_ref[j, 0, r]
                hi_row = md_ref[j, 1, r]
                out.append(merged(
                    lambda c, n: src[0, lo_row, pl.ds(c, n), :],
                    lambda c, n: src[1, hi_row, pl.ds(c, n), :],
                    md_ref[j, 2, r], span, c0, size,
                ))
            for i in range(SUB):
                r = g * SUB + i
                if j + 1 < flevels:
                    put(j + 1, k, r, c0, size, out[i])
                else:
                    fin[pl.ds(pl.multiple_of(r * SUB, SUB), SUB), :] = out[i]

        rows(body)

    def prefix(c0):
        sums = jnp.dot(
            fin[...], tri[...], precision=lax.Precision.HIGHEST,
            preferred_element_type=jnp.float32,
        )
        own = sums[:, :LANES].reshape(channels, SUB, LANES)
        eb[:, pl.ds(c0, SUB), :] = own
        return own, sums[:, LANES:].reshape(channels, SUB, LANES)

    def boxcar(c0):
        own, total = prefix(c0)
        far = total + eb[:, pl.ds(c0 + 1, SUB), :]
        lanes = lax.broadcasted_iota(jnp.int32, (channels, SUB, LANES), 2)

        def body(i, best):
            wide = w_ref[i]
            mixed = jnp.where(lanes < wide, far, own)
            ahead = pltpu.roll(mixed, LANES - wide, 2)
            return jnp.maximum(best, (ahead - own) * scl[i][None])

        best = lax.fori_loop(
            0, nwidth, body, jnp.full((channels, SUB, LANES), -jnp.inf, jnp.float32)
        )
        for r in range(channels):
            at = (r // SUB) * chunks * SUB + c0 * SUB + r % SUB
            o_ref[pl.ds(at, SUB, stride=SUB), :] = best[r]

    halo_size = -(-halo_chunks // SUB) * SUB
    pieces = [(chunks - tile * (k + 1), tile) for k in range(count)]

    def tiles(k):
        found = [(pieces[k][0], tile, False)]
        if k == 0:
            found.insert(0, (chunks, halo_size, True))
        return found

    copies = {}
    for j in range(flevels):
        for k in range(count):
            size = tile
            if k == 0:
                size = size + halo_chunks
            window = bufs[j][k].at[sides[j], :, pl.ds(0, size), :]
            copies[j, k] = pltpu.make_async_remote_copy(
                src_ref=window, dst_ref=window,
                send_sem=bsend.at[j, k], recv_sem=brecv.at[j, k],
                device_id=partners[j], device_id_type=MESH,
            )

    def local_stage(k):
        for c0, size, is_halo in tiles(k):
            normalise(c0, size, is_halo)
            for s in range(llevels):
                local_level(s, k, c0, size)
        copies[0, k].start()

    def merge_stage(j, k):
        copies[j, k].wait_recv()
        if k:
            over = channels * 2**j // LANES + 1
            bufs[j][k][:, :, pl.ds(tile, over), :] = bufs[j][k - 1][:, :, pl.ds(0, over), :]
        for c0, size, is_halo in tiles(k):
            rel = c0 - pieces[k][0]
            if j + 1 < flevels:
                merge_level(j, k, rel, size)
            elif is_halo:
                merge_level(j, k, rel, SUB)
                prefix(c0)
            else:
                for sub in reversed(range(size // SUB)):
                    merge_level(j, k, rel + sub * SUB, SUB)
                    boxcar(c0 + sub * SUB)
        if j + 1 < flevels:
            copies[j + 1, k].start()

    lags = [FIRST_LAG] + [MID_LAG] * (flevels - 2) + [LAST_LAG]
    behind = [sum(lags[: j + 1]) for j in range(flevels)]
    for step in range(count + behind[-1]):
        if step < count:
            local_stage(step)
        for j in range(flevels):
            if 0 <= step - behind[j] < count:
                merge_stage(j, step - behind[j])

    stat_copy.wait_send()
    for copy in halo_copies:
        copy.wait_send()
    for copy in copies.values():
        copy.wait_send()


def per_device(mesh_shape, spectra, local_delays, merge_delays, widths):
    channels, block_len = spectra.shape
    freq_count = mesh_shape["freq"]
    chunks = block_len // LANES
    groups = channels // SUB
    tile = SUB
    halo_chunks = -(-(channels * freq_count - 1 + LANES) // LANES)
    halo_size = -(-halo_chunks // SUB) * SUB
    over = -(-(channels * freq_count // 2 // LANES + 1) // SUB) * SUB
    depth = chunks + halo_size + SUB
    llevels = channels.bit_length() - 1
    flevels = freq_count.bit_length() - 1
    count = chunks // tile
    f32 = jnp.float32
    flat = spectra.reshape(groups, SUB, chunks, LANES).transpose(0, 2, 1, 3)
    flat = flat.reshape(groups * chunks * SUB, LANES)
    smem = pl.BlockSpec(memory_space=pltpu.SMEM)
    vmem = pl.BlockSpec(memory_space=pltpu.VMEM)
    dma = pltpu.SemaphoreType.DMA
    out = pl.pallas_call(
        functools.partial(kernel, (channels, chunks, freq_count, halo_chunks, tile)),
        out_shape=jax.ShapeDtypeStruct(flat.shape, f32),
        in_specs=[vmem, smem, smem, smem],
        out_specs=vmem,
        scratch_shapes=[
            pltpu.VMEM((groups, halo_chunks * SUB, LANES), f32),
            pltpu.VMEM((2, channels, LANES), f32),
            pltpu.VMEM((2, channels, LANES), f32),
            pltpu.VMEM((2, channels, LANES), f32),
            pltpu.VMEM((channels * SUB, LANES), f32),
            pltpu.VMEM((channels, depth, LANES), f32),
            pltpu.VMEM((LANES, 2 * LANES), f32),
            pltpu.VMEM((widths.shape[0], SUB, LANES), f32),
        ]
        + [pltpu.VMEM((channels, depth, LANES), f32)] * llevels
        + ([pltpu.VMEM((2, channels, tile + halo_size + over, LANES), f32)]
           + [pltpu.VMEM((2, channels, tile + over, LANES), f32)] * (count - 1)) * flevels
        + [
            dma((groups,)), dma((groups,)), dma, dma,
            dma((flevels, count)), dma((flevels, count)),
        ],
        compiler_params=pltpu.CompilerParams(
            collective_id=0, has_side_effects=True, vmem_limit_bytes=56 * 2**20
        ),
    )(flat, local_delays, merge_delays, widths)
    out = out.reshape(groups, chunks, SUB, LANES).transpose(0, 2, 1, 3)
    return out.reshape(channels, block_len)


def solution(mesh):
    placed = (P(("beam", "freq"), "tm"), P(None, None, "freq"), P(None, None, "freq"), P())
    return jax.shard_map(
        functools.partial(per_device, dict(mesh.shape)), mesh=mesh, in_specs=placed,
        out_specs=P(("beam", "freq"), "tm"), check_vma=False,
    )
```

```python
import functools
import math

import jax
import jax.numpy as jnp
from jax import lax
from jax.experimental import pallas as pl
from jax.experimental.pallas import tpu as pltpu
from jax.sharding import PartitionSpec as P

WMAX = 32
EPSILON = 1e-05
LANES = 128
SUB = 8
MESH = pl.DeviceIdType.MESH
FIRST_LAG = 1
MID_LAG = 1
LAST_LAG = 3
UNROLL = 16


def kernel(geo, x_ref, ld_ref, md_ref, w_ref, o_ref, *scratch):
    channels, chunks, freq_count, halo_chunks, tile = geo
    groups = channels // SUB
    llevels = channels.bit_length() - 1
    flevels = freq_count.bit_length() - 1
    samples = chunks * LANES
    nwidth = w_ref.shape[0]
    halo, st_own, st_peer, nrm, fin, eb, tri, scl = scratch[:8]
    loc = scratch[8 : 8 + llevels]
    count = chunks // tile
    flat_bufs = scratch[8 + llevels : 8 + llevels + flevels * count]
    bufs = [flat_bufs[j * count : (j + 1) * count] for j in range(flevels)]
    hsend, hrecv, ssend, srecv, bsend, brecv = scratch[8 + llevels + flevels * count :]

    tm = lax.axis_index("tm")
    freq = lax.axis_index("freq")
    peer = {"tm": 1 - tm}
    sides, partners = [], []
    for j in range(flevels):
        stride = 2**j
        side = (freq // stride) % 2
        sides.append(side)
        partners.append({"freq": freq + stride - 2 * stride * side})

    barrier = pltpu.get_barrier_semaphore()
    for other in [peer] + partners:
        pl.semaphore_signal(barrier, inc=1, device_id=other, device_id_type=MESH)

    lane = lax.broadcasted_iota(jnp.int32, (SUB, LANES), 1)

    for g in range(groups):
        block = x_ref[pl.ds(g * chunks * SUB, chunks * SUB), :].reshape(chunks, SUB, LANES)
        mean = jnp.sum(jnp.sum(block, axis=0), axis=1, keepdims=True) / samples
        off = block - mean[None]
        square = jnp.sum(jnp.sum(off * off, axis=0), axis=1, keepdims=True)
        st_own[0, pl.ds(g * SUB, SUB), :] = jnp.broadcast_to(mean, (SUB, LANES))
        st_own[1, pl.ds(g * SUB, SUB), :] = jnp.broadcast_to(square, (SUB, LANES))

    pl.semaphore_wait(barrier, 1 + flevels)
    stat_copy = pltpu.make_async_remote_copy(
        src_ref=st_own, dst_ref=st_peer, send_sem=ssend, recv_sem=srecv,
        device_id=peer, device_id_type=MESH,
    )
    stat_copy.start()
    halo_copies = []
    for g in range(groups):
        copy = pltpu.make_async_remote_copy(
            src_ref=x_ref.at[pl.ds(g * chunks * SUB, halo_chunks * SUB), :],
            dst_ref=halo.at[g],
            send_sem=hsend.at[g], recv_sem=hrecv.at[g],
            device_id=peer, device_id_type=MESH,
        )
        copy.start()
        halo_copies.append(copy)

    before = lax.broadcasted_iota(jnp.int32, (LANES, 2 * LANES), 0)
    after = lax.broadcasted_iota(jnp.int32, (LANES, 2 * LANES), 1)
    tri[...] = jnp.where(before < after, 1.0, 0.0)
    norm = 1.0 / math.sqrt(channels * freq_count)
    for i in range(nwidth):
        wide = jnp.full((SUB, LANES), w_ref[i].astype(jnp.float32), jnp.float32)
        scl[i] = (1.0 / jnp.sqrt(wide)) * norm

    stat_copy.wait_recv()
    mean_a, mean_b = st_own[0], st_peer[0]
    gap = mean_a - mean_b
    variance = (st_own[1] + st_peer[1] + gap * gap * (samples / 2)) / (2 * samples)
    nrm[0] = (mean_a + mean_b) * 0.5
    nrm[1] = 1.0 / jnp.sqrt(variance + EPSILON)
    for copy in halo_copies:
        copy.wait_recv()

    keep = jnp.where(tm == 0, 1.0, 0.0)

    def rows(body):
        for g in range(groups):
            body(g)

    def normalise(c0, size, is_halo):
        def body(g):
            out = []
            for i in range(SUB):
                r = g * SUB + i
                if is_halo:
                    part = halo[g, pl.ds(i, halo_chunks, stride=SUB), :]
                    gain = nrm[1, pl.ds(r, 1), :] * keep
                else:
                    part = x_ref[pl.ds(g * chunks * SUB + c0 * SUB + i, size, stride=SUB), :]
                    gain = nrm[1, pl.ds(r, 1), :]
                out.append((part - nrm[0, pl.ds(r, 1), :]) * gain)
            for i in range(SUB):
                r = g * SUB + i
                count = halo_chunks if is_halo else size
                loc[0][r, pl.ds(c0, count), :] = out[i]

        rows(body)

    def merged(low, high, lag, span, c0, size):
        if span < LANES:
            jump = 0
        else:
            jump = lag // LANES
            lag = lag % LANES
        cur = high(c0 + jump, size)
        nxt = high(c0 + jump + 1, size)
        lanes = lax.broadcasted_iota(jnp.int32, (size, LANES), 1)
        mixed = jnp.where(lanes < lag, nxt, cur)
        return low(c0, size) + pltpu.roll(mixed, (LANES - lag) % LANES, 1)

    def put(level, k, r, rel, size, value):
        bufs[level][k][sides[level], r, pl.ds(rel, size), :] = value

    def local_level(s, k, c0, size):
        span = 2**s
        src = loc[s]

        def body(g):
            out = []
            for i in range(SUB):
                r = g * SUB + i
                base = (r // (2 * span)) * (2 * span)
                lo_row = base + ld_ref[0, s, r]
                hi_row = base + span + ld_ref[1, s, r]
                out.append(merged(
                    lambda c, n: src[lo_row, pl.ds(c, n), :],
                    lambda c, n: src[hi_row, pl.ds(c, n), :],
                    ld_ref[2, s, r], span, c0, size,
                ))
            for i in range(SUB):
                r = g * SUB + i
                if s + 1 < llevels:
                    loc[s + 1][r, pl.ds(c0, size), :] = out[i]
                else:
                    put(0, k, r, c0 - pieces[k][0], size, out[i])

        rows(body)

    def merge_level(j, k, c0, size):
        span = channels * 2**j
        src = bufs[j][k]

        def body(g):
            out = []
            for i in range(SUB):
                r = g * SUB + i
                lo_row = md_ref[j, 0, r]
                hi_row = md_ref[j, 1, r]
                out.append(merged(
                    lambda c, n: src[0, lo_row, pl.ds(c, n), :],
                    lambda c, n: src[1, hi_row, pl.ds(c, n), :],
                    md_ref[j, 2, r], span, c0, size,
                ))
            for i in range(SUB):
                r = g * SUB + i
                if j + 1 < flevels:
                    put(j + 1, k, r, c0, size, out[i])
                else:
                    fin[pl.ds(pl.multiple_of(r * SUB, SUB), SUB), :] = out[i]

        rows(body)

    def prefix(c0):
        sums = jnp.dot(
            fin[...], tri[...], precision=lax.Precision.HIGHEST,
            preferred_element_type=jnp.float32,
        )
        own = sums[:, :LANES].reshape(channels, SUB, LANES)
        eb[:, pl.ds(c0, SUB), :] = own
        return own, sums[:, LANES:].reshape(channels, SUB, LANES)

    def boxcar(c0):
        own, total = prefix(c0)
        far = total + eb[:, pl.ds(c0 + 1, SUB), :]
        lanes = lax.broadcasted_iota(jnp.int32, (channels, SUB, LANES), 2)

        def body(at, best):
            for u in range(unroll):
                i = at * unroll + u
                wide = w_ref[i]
                mixed = jnp.where(lanes < wide, far, own)
                ahead = pltpu.roll(mixed, LANES - wide, 2)
                best = jnp.maximum(best, (ahead - own) * scl[i][None])
            return best

        unroll = math.gcd(nwidth, UNROLL)
        best = lax.fori_loop(
            0, nwidth // unroll, body, jnp.full((channels, SUB, LANES), -jnp.inf, jnp.float32)
        )
        for r in range(channels):
            at = (r // SUB) * chunks * SUB + c0 * SUB + r % SUB
            o_ref[pl.ds(at, SUB, stride=SUB), :] = best[r]

    halo_size = -(-halo_chunks // SUB) * SUB
    pieces = [(chunks - tile * (k + 1), tile) for k in range(count)]

    def tiles(k):
        found = [(pieces[k][0], tile, False)]
        if k == 0:
            found.insert(0, (chunks, halo_size, True))
        return found

    copies = {}
    for j in range(flevels):
        for k in range(count):
            size = tile
            if k == 0:
                size = size + halo_chunks
            window = bufs[j][k].at[sides[j], :, pl.ds(0, size), :]
            copies[j, k] = pltpu.make_async_remote_copy(
                src_ref=window, dst_ref=window,
                send_sem=bsend.at[j, k], recv_sem=brecv.at[j, k],
                device_id=partners[j], device_id_type=MESH,
            )

    def local_stage(k):
        for c0, size, is_halo in tiles(k):
            normalise(c0, size, is_halo)
            for s in range(llevels):
                local_level(s, k, c0, size)
        copies[0, k].start()

    def merge_stage(j, k):
        copies[j, k].wait_recv()
        if k:
            over = channels * 2**j // LANES + 1
            bufs[j][k][:, :, pl.ds(tile, over), :] = bufs[j][k - 1][:, :, pl.ds(0, over), :]
        for c0, size, is_halo in tiles(k):
            rel = c0 - pieces[k][0]
            if j + 1 < flevels:
                merge_level(j, k, rel, size)
            elif is_halo:
                merge_level(j, k, rel, SUB)
                prefix(c0)
            else:
                for sub in reversed(range(size // SUB)):
                    merge_level(j, k, rel + sub * SUB, SUB)
                    boxcar(c0 + sub * SUB)
        if j + 1 < flevels:
            copies[j + 1, k].start()

    lags = [FIRST_LAG] + [MID_LAG] * (flevels - 2) + [LAST_LAG]
    behind = [sum(lags[: j + 1]) for j in range(flevels)]
    for step in range(count + behind[-1]):
        if step < count:
            local_stage(step)
        for j in range(flevels):
            if 0 <= step - behind[j] < count:
                merge_stage(j, step - behind[j])

    stat_copy.wait_send()
    for copy in halo_copies:
        copy.wait_send()
    for copy in copies.values():
        copy.wait_send()


def per_device(mesh_shape, spectra, local_delays, merge_delays, widths):
    channels, block_len = spectra.shape
    freq_count = mesh_shape["freq"]
    chunks = block_len // LANES
    groups = channels // SUB
    tile = SUB
    halo_chunks = -(-(channels * freq_count - 1 + LANES) // LANES)
    halo_size = -(-halo_chunks // SUB) * SUB
    over = -(-(channels * freq_count // 2 // LANES + 1) // SUB) * SUB
    depth = chunks + halo_size + SUB
    llevels = channels.bit_length() - 1
    flevels = freq_count.bit_length() - 1
    count = chunks // tile
    f32 = jnp.float32
    flat = spectra.reshape(groups, SUB, chunks, LANES).transpose(0, 2, 1, 3)
    flat = flat.reshape(groups * chunks * SUB, LANES)
    smem = pl.BlockSpec(memory_space=pltpu.SMEM)
    vmem = pl.BlockSpec(memory_space=pltpu.VMEM)
    dma = pltpu.SemaphoreType.DMA
    out = pl.pallas_call(
        functools.partial(kernel, (channels, chunks, freq_count, halo_chunks, tile)),
        out_shape=jax.ShapeDtypeStruct(flat.shape, f32),
        in_specs=[vmem, smem, smem, smem],
        out_specs=vmem,
        scratch_shapes=[
            pltpu.VMEM((groups, halo_chunks * SUB, LANES), f32),
            pltpu.VMEM((2, channels, LANES), f32),
            pltpu.VMEM((2, channels, LANES), f32),
            pltpu.VMEM((2, channels, LANES), f32),
            pltpu.VMEM((channels * SUB, LANES), f32),
            pltpu.VMEM((channels, depth, LANES), f32),
            pltpu.VMEM((LANES, 2 * LANES), f32),
            pltpu.VMEM((widths.shape[0], SUB, LANES), f32),
        ]
        + [pltpu.VMEM((channels, depth, LANES), f32)] * llevels
        + ([pltpu.VMEM((2, channels, tile + halo_size + over, LANES), f32)]
           + [pltpu.VMEM((2, channels, tile + over, LANES), f32)] * (count - 1)) * flevels
        + [
            dma((groups,)), dma((groups,)), dma, dma,
            dma((flevels, count)), dma((flevels, count)),
        ],
        compiler_params=pltpu.CompilerParams(
            collective_id=0, has_side_effects=True, vmem_limit_bytes=56 * 2**20
        ),
    )(flat, local_delays.transpose(1, 0, 2), merge_delays, widths)
    out = out.reshape(groups, chunks, SUB, LANES).transpose(0, 2, 1, 3)
    return out.reshape(channels, block_len)


def solution(mesh):
    placed = (P(("beam", "freq"), "tm"), P(None, None, "freq"), P(None, None, "freq"), P())
    return jax.shard_map(
        functools.partial(per_device, dict(mesh.shape)), mesh=mesh, in_specs=placed,
        out_specs=P(("beam", "freq"), "tm"), check_vma=False,
    )
```

```python
import functools
import math

import jax
import jax.numpy as jnp
from jax import lax
from jax.experimental import pallas as pl
from jax.experimental.pallas import tpu as pltpu
from jax.sharding import PartitionSpec as P

WMAX = 32
EPSILON = 1e-05
LANES = 128
SUB = 8
MESH = pl.DeviceIdType.MESH
FIRST_LAG = 1
MID_LAG = 1
LAST_LAG = 3
UNROLL = 16


def kernel(geo, x_ref, ld_ref, md_ref, w_ref, o_ref, *scratch):
    channels, chunks, freq_count, halo_chunks, tile = geo
    groups = channels // SUB
    llevels = channels.bit_length() - 1
    flevels = freq_count.bit_length() - 1
    samples = chunks * LANES
    nwidth = w_ref.shape[0]
    halo, st_own, st_peer, nrm, fin, eb, tri, scl = scratch[:8]
    loc = scratch[8 : 8 + llevels]
    count = chunks // tile
    flat_bufs = scratch[8 + llevels : 8 + llevels + flevels * count]
    bufs = [flat_bufs[j * count : (j + 1) * count] for j in range(flevels)]
    hsend, hrecv, ssend, srecv, bsend, brecv = scratch[8 + llevels + flevels * count :]

    tm = lax.axis_index("tm")
    freq = lax.axis_index("freq")
    peer = {"tm": 1 - tm}
    sides, partners = [], []
    for j in range(flevels):
        stride = 2**j
        side = (freq // stride) % 2
        sides.append(side)
        partners.append({"freq": freq + stride - 2 * stride * side})

    barrier = pltpu.get_barrier_semaphore()
    for other in [peer] + partners:
        pl.semaphore_signal(barrier, inc=1, device_id=other, device_id_type=MESH)

    lane = lax.broadcasted_iota(jnp.int32, (SUB, LANES), 1)

    for g in range(groups):
        block = x_ref[pl.ds(g * chunks * SUB, chunks * SUB), :].reshape(chunks, SUB, LANES)
        mean = jnp.sum(jnp.sum(block, axis=0), axis=1, keepdims=True) / samples
        off = block - mean[None]
        square = jnp.sum(jnp.sum(off * off, axis=0), axis=1, keepdims=True)
        st_own[0, pl.ds(g * SUB, SUB), :] = jnp.broadcast_to(mean, (SUB, LANES))
        st_own[1, pl.ds(g * SUB, SUB), :] = jnp.broadcast_to(square, (SUB, LANES))

    pl.semaphore_wait(barrier, 1 + flevels)
    stat_copy = pltpu.make_async_remote_copy(
        src_ref=st_own, dst_ref=st_peer, send_sem=ssend, recv_sem=srecv,
        device_id=peer, device_id_type=MESH,
    )
    stat_copy.start()
    halo_copies = []
    for g in range(groups):
        copy = pltpu.make_async_remote_copy(
            src_ref=x_ref.at[pl.ds(g * chunks * SUB, halo_chunks * SUB), :],
            dst_ref=halo.at[g],
            send_sem=hsend.at[g], recv_sem=hrecv.at[g],
            device_id=peer, device_id_type=MESH,
        )
        copy.start()
        halo_copies.append(copy)

    before = lax.broadcasted_iota(jnp.int32, (LANES, 2 * LANES), 0)
    after = lax.broadcasted_iota(jnp.int32, (LANES, 2 * LANES), 1)
    tri[...] = jnp.where(before < after, 1.0, 0.0)
    norm = 1.0 / math.sqrt(channels * freq_count)
    for i in range(nwidth):
        wide = jnp.full((SUB, LANES), w_ref[i].astype(jnp.float32), jnp.float32)
        scl[i] = (1.0 / jnp.sqrt(wide)) * norm

    stat_copy.wait_recv()
    mean_a, mean_b = st_own[0], st_peer[0]
    gap = mean_a - mean_b
    variance = (st_own[1] + st_peer[1] + gap * gap * (samples / 2)) / (2 * samples)
    nrm[0] = (mean_a + mean_b) * 0.5
    nrm[1] = 1.0 / jnp.sqrt(variance + EPSILON)
    for copy in halo_copies:
        copy.wait_recv()

    keep = jnp.where(tm == 0, 1.0, 0.0)

    def rows(body):
        for g in range(groups):
            body(g)

    def normalise(c0, size, is_halo):
        def body(g):
            out = []
            for i in range(SUB):
                r = g * SUB + i
                if is_halo:
                    part = halo[g, pl.ds(i, halo_chunks, stride=SUB), :]
                    gain = nrm[1, pl.ds(r, 1), :] * keep
                else:
                    part = x_ref[pl.ds(g * chunks * SUB + c0 * SUB + i, size, stride=SUB), :]
                    gain = nrm[1, pl.ds(r, 1), :]
                out.append((part - nrm[0, pl.ds(r, 1), :]) * gain)
            for i in range(SUB):
                r = g * SUB + i
                count = halo_chunks if is_halo else size
                loc[0][r, pl.ds(c0, count), :] = out[i]

        rows(body)

    def merged(low, high, lag, span, c0, size):
        if span < LANES:
            jump = 0
        else:
            jump = lag // LANES
            lag = lag % LANES
        cur = high(c0 + jump, size)
        nxt = high(c0 + jump + 1, size)
        lanes = lax.broadcasted_iota(jnp.int32, (size, LANES), 1)
        mixed = jnp.where(lanes < lag, nxt, cur)
        return low(c0, size) + pltpu.roll(mixed, (LANES - lag) % LANES, 1)

    def put(level, k, r, rel, size, value):
        bufs[level][k][sides[level], r, pl.ds(rel, size), :] = value

    def local_level(s, k, c0, size):
        span = 2**s
        src = loc[s]

        def body(g):
            out = []
            for i in range(SUB):
                r = g * SUB + i
                base = (r // (2 * span)) * (2 * span)
                lo_row = base + ld_ref[0, s, r]
                hi_row = base + span + ld_ref[1, s, r]
                out.append(merged(
                    lambda c, n: src[lo_row, pl.ds(c, n), :],
                    lambda c, n: src[hi_row, pl.ds(c, n), :],
                    ld_ref[2, s, r], span, c0, size,
                ))
            for i in range(SUB):
                r = g * SUB + i
                if s + 1 < llevels:
                    loc[s + 1][r, pl.ds(c0, size), :] = out[i]
                else:
                    put(0, k, r, c0 - pieces[k][0], size, out[i])

        rows(body)

    def merge_level(j, k, c0, size):
        span = channels * 2**j
        src = bufs[j][k]

        def body(g):
            out = []
            for i in range(SUB):
                r = g * SUB + i
                lo_row = md_ref[j, 0, r]
                hi_row = md_ref[j, 1, r]
                out.append(merged(
                    lambda c, n: src[0, lo_row, pl.ds(c, n), :],
                    lambda c, n: src[1, hi_row, pl.ds(c, n), :],
                    md_ref[j, 2, r], span, c0, size,
                ))
            for i in range(SUB):
                r = g * SUB + i
                if j + 1 < flevels:
                    put(j + 1, k, r, c0, size, out[i])
                else:
                    fin[pl.ds(pl.multiple_of(r * SUB, SUB), SUB), :] = out[i]

        rows(body)

    def prefix(c0):
        sums = jnp.dot(
            fin[...], tri[...], precision=lax.Precision.HIGHEST,
            preferred_element_type=jnp.float32,
        )
        own = sums[:, :LANES].reshape(channels, SUB, LANES)
        eb[:, pl.ds(c0, SUB), :] = own
        return own, sums[:, LANES:].reshape(channels, SUB, LANES)

    def boxcar(c0):
        own, total = prefix(c0)
        far = total + eb[:, pl.ds(c0 + 1, SUB), :]
        lanes = lax.broadcasted_iota(jnp.int32, (channels, SUB, LANES), 2)

        def body(at, best):
            for u in range(unroll):
                i = at * unroll + u
                wide = w_ref[i]
                mixed = jnp.where(lanes < wide, far, own)
                ahead = pltpu.roll(mixed, LANES - wide, 2)
                best = jnp.maximum(best, (ahead - own) * scl[i][None])
            return best

        unroll = math.gcd(nwidth, UNROLL)
        best = lax.fori_loop(
            0, nwidth // unroll, body, jnp.full((channels, SUB, LANES), -jnp.inf, jnp.float32)
        )
        for r in range(channels):
            at = (r // SUB) * chunks * SUB + c0 * SUB + r % SUB
            o_ref[pl.ds(at, SUB, stride=SUB), :] = best[r]

    halo_size = -(-halo_chunks // SUB) * SUB
    pieces = [(chunks - tile * (k + 1), tile) for k in range(count)]

    def tiles(k):
        found = [(pieces[k][0], tile, False)]
        if k == 0:
            found.insert(0, (chunks, halo_size, True))
        return found

    copies = {}
    for j in range(flevels):
        for k in range(count):
            size = tile
            if k == 0:
                size = size + halo_chunks
            window = bufs[j][k].at[sides[j], :, pl.ds(0, size), :]
            copies[j, k] = pltpu.make_async_remote_copy(
                src_ref=window, dst_ref=window,
                send_sem=bsend.at[j, k], recv_sem=brecv.at[j, k],
                device_id=partners[j], device_id_type=MESH,
            )

    def local_stage(k):
        for c0, size, is_halo in tiles(k):
            normalise(c0, size, is_halo)
            for s in range(llevels):
                local_level(s, k, c0, size)
        copies[0, k].start()

    def merge_stage(j, k):
        copies[j, k].wait_recv()
        if k:
            over = channels * 2**j // LANES + 1
            bufs[j][k][:, :, pl.ds(tile, over), :] = bufs[j][k - 1][:, :, pl.ds(0, over), :]
        for c0, size, is_halo in tiles(k):
            rel = c0 - pieces[k][0]
            if j + 1 < flevels:
                merge_level(j, k, rel, size)
            elif is_halo:
                merge_level(j, k, rel, SUB)
                prefix(c0)
            else:
                for sub in reversed(range(size // SUB)):
                    merge_level(j, k, rel + sub * SUB, SUB)
                    boxcar(c0 + sub * SUB)
        if j + 1 < flevels:
            copies[j + 1, k].start()

    lags = [FIRST_LAG] + [MID_LAG] * (flevels - 2) + [LAST_LAG]
    behind = [sum(lags[: j + 1]) for j in range(flevels)]
    for step in range(count + behind[-1]):
        if step < count:
            local_stage(step)
        for j in range(flevels):
            if 0 <= step - behind[j] < count:
                merge_stage(j, step - behind[j])

    stat_copy.wait_send()
    for copy in halo_copies:
        copy.wait_send()
    for copy in copies.values():
        copy.wait_send()


def per_device(mesh_shape, spectra, local_delays, merge_delays, widths):
    channels, block_len = spectra.shape
    freq_count = mesh_shape["freq"]
    chunks = block_len // LANES
    groups = channels // SUB
    tile = SUB
    halo_chunks = -(-(channels * freq_count - 1 + LANES) // LANES)
    halo_size = -(-halo_chunks // SUB) * SUB
    over = -(-(channels * freq_count // 2 // LANES + 1) // SUB) * SUB
    depth = chunks + halo_size + SUB
    llevels = channels.bit_length() - 1
    flevels = freq_count.bit_length() - 1
    count = chunks // tile
    f32 = jnp.float32
    flat = spectra.reshape(groups, SUB, chunks, LANES).transpose(0, 2, 1, 3)
    flat = flat.reshape(groups * chunks * SUB, LANES)
    smem = pl.BlockSpec(memory_space=pltpu.SMEM)
    vmem = pl.BlockSpec(memory_space=pltpu.VMEM)
    dma = pltpu.SemaphoreType.DMA
    out = pl.pallas_call(
        functools.partial(kernel, (channels, chunks, freq_count, halo_chunks, tile)),
        out_shape=pltpu.VMEM(flat.shape, f32),
        in_specs=[vmem, smem, smem, smem],
        out_specs=vmem,
        scratch_shapes=[
            pltpu.VMEM((groups, halo_chunks * SUB, LANES), f32),
            pltpu.VMEM((2, channels, LANES), f32),
            pltpu.VMEM((2, channels, LANES), f32),
            pltpu.VMEM((2, channels, LANES), f32),
            pltpu.VMEM((channels * SUB, LANES), f32),
            pltpu.VMEM((channels, depth, LANES), f32),
            pltpu.VMEM((LANES, 2 * LANES), f32),
            pltpu.VMEM((widths.shape[0], SUB, LANES), f32),
        ]
        + [pltpu.VMEM((channels, depth, LANES), f32)] * llevels
        + ([pltpu.VMEM((2, channels, tile + halo_size + over, LANES), f32)]
           + [pltpu.VMEM((2, channels, tile + over, LANES), f32)] * (count - 1)) * flevels
        + [
            dma((groups,)), dma((groups,)), dma, dma,
            dma((flevels, count)), dma((flevels, count)),
        ],
        compiler_params=pltpu.CompilerParams(
            collective_id=0, has_side_effects=True, vmem_limit_bytes=56 * 2**20
        ),
    )(flat, local_delays.transpose(1, 0, 2), merge_delays, widths)
    out = out.reshape(groups, chunks, SUB, LANES).transpose(0, 2, 1, 3)
    return out.reshape(channels, block_len)


def solution(mesh):
    placed = (P(("beam", "freq"), "tm"), P(None, None, "freq"), P(None, None, "freq"), P())
    return jax.shard_map(
        functools.partial(per_device, dict(mesh.shape)), mesh=mesh, in_specs=placed,
        out_specs=P(("beam", "freq"), "tm"), check_vma=False,
    )
```
